32 devices in a mesh: depth: 8 (over z, x), stripe: 4 (over y, core).
Axes of the slice: x: 2, y: 2, z: 4, core: 2. Of those that a mesh axis runs over, the one named last changes fastest.
Arguments:
- object_slices: float32 [8, 2, 1024, 384], P('depth', None, 'stripe'), may hold values from -1 to 1, as said below
- probe_wave: bfloat16 [2, 256, 256], replicated, may hold values from -5 to 5
- amplitudes: bfloat16 [16, 256, 256], P('stripe'), may hold values from 0 to 2
- positions: int32 [16, 2], replicated, may hold values from 0 to 255, as said below
- counts: int32 [4], replicated, may hold values from 1 to 4, as said below
Outputs:
- grad_object: float32 [8, 2, 1024, 384], P('depth', None, 'stripe')
The draws below stay inside these ranges and needn't reach their ends.
Inputs may be any that keep to these rules, and one draw needn't show every extreme that they name: `object_slices`: every cell has magnitude at most 1. `positions`: row offsets lie in 0 to 255 and column offsets in 0 to 128. The counts sum to 8 and the largest equals 4; a stripe's live slots are its first ones.
All inputs are finite; a program needn't handle non-finite values.
Results may differ from the reference program's by a relative error of at most 0.0003.
Values may be sent and summed in bfloat16 or wider, within the bound.
A program may use at most 64 MiB of HBM per device.

```python
import math
import jax
import jax.numpy as jnp
from jax import lax

WIN = 256
STRIPE_ROWS = 256
W = 384
CAP = 4
SLICES = 8
ROWS_ALL = 1024
SLOTS = 16
TOTAL = 8
N_STRIPE = 4


def draw_object_slices(key, part):
    key_mag, key_phase = jax.random.split(jax.random.fold_in(key, 11))
    shape = (SLICES, ROWS_ALL, W)
    magnitude = jax.random.uniform(key_mag, shape, jnp.float32, 0.97, 1.0)
    phase_angle = jax.random.uniform(key_phase, shape, jnp.float32, -math.pi, math.pi)
    return jnp.stack([magnitude * jnp.cos(phase_angle), magnitude * jnp.sin(phase_angle)], axis=1).astype(jnp.float32)


def draw_positions(key, part):
    key_row, key_col, key_cross = jax.random.split(jax.random.fold_in(key, 23), 3)
    rows_drawn = jax.random.randint(key_row, (SLOTS,), 0, STRIPE_ROWS, jnp.int32)
    cols_drawn = jax.random.randint(key_col, (SLOTS,), 0, W - WIN + 1, jnp.int32)
    crossing = jax.random.randint(key_cross, (N_STRIPE,), STRIPE_ROWS - WIN // 2, STRIPE_ROWS, jnp.int32)
    first_slots = jnp.arange(N_STRIPE, dtype=jnp.int32) * CAP
    rows_drawn = rows_drawn.at[first_slots].set(crossing)
    rows_drawn = rows_drawn.at[0].set(STRIPE_ROWS - 1)
    cols_drawn = cols_drawn.at[0].set(W - WIN).at[1].set(0)
    return jnp.stack([rows_drawn, cols_drawn], axis=1).astype(jnp.int32)


def draw_counts(key, part):
    key_fill, key_turn = jax.random.split(jax.random.fold_in(key, 37))
    spare_units = (N_STRIPE - 1) * (CAP - 1)
    drawn_units = TOTAL - CAP - (N_STRIPE - 1)
    unit_order = jax.random.permutation(key_fill, spare_units)
    chosen = unit_order[:drawn_units] // (CAP - 1)
    added_units = jnp.sum((chosen[:, None] == jnp.arange(N_STRIPE - 1, dtype=jnp.int32)[None, :]).astype(jnp.int32), axis=0)
    rest_counts = (1 + added_units).astype(jnp.int32)
    full_counts = jnp.concatenate([jnp.full((1,), CAP, jnp.int32), rest_counts])
    rotation = jax.random.randint(key_turn, (), 0, N_STRIPE, jnp.int32)
    return jnp.roll(full_counts, rotation).astype(jnp.int32)


def levels(rng, dims, pieces, smallest, largest):
    gain, own = 1.0, jax.random.fold_in(rng, 6)
    for position, blocks in pieces:
        heights = jnp.exp(jax.random.uniform(jax.random.fold_in(own, position), (blocks,), jnp.float32, smallest / len(pieces), largest / len(pieces)))
        gain = gain * jnp.repeat(heights, dims[position] // blocks).reshape([-1 if axis == position else 1 for axis in range(len(dims))])
    return gain


def bell_draw(own_key, extent, scale, most, kind=jnp.bfloat16):
    values = scale * jax.random.normal(own_key, extent, jnp.float32)
    return jnp.clip(values, min=-most, max=most).astype(kind)


def setup_inputs(seed: int = 0) -> dict:
    streams_of = jax.random.split(jax.random.key(seed), 6)
    object_slices = draw_object_slices(jax.random.fold_in(streams_of[5], 71), 0)
    probe_wave = bell_draw(streams_of[1], (2, WIN, WIN), 0.7, 5.0)
    amplitudes = jnp.clip(2.0 * jax.random.uniform(streams_of[2], (SLOTS, WIN, WIN), jnp.float32) ** levels(streams_of[2], (SLOTS, WIN, WIN), ((0, 4),), -0.2, 0.2), 0.0, 2.0).astype(jnp.bfloat16)
    positions = draw_positions(jax.random.fold_in(streams_of[5], 71), 0)
    counts = draw_counts(jax.random.fold_in(streams_of[5], 71), 0)
    return {"object_slices": object_slices, "probe_wave": probe_wave, "amplitudes": amplitudes, "positions": positions, "counts": counts}


smoothing = 0.25
highest = lax.Precision.HIGHEST

def make_tables(length):
    index_row = jnp.arange(length, dtype=jnp.int32)
    product = index_row[:, None] * index_row[None, :] % length
    angle = 2.0 * math.pi * product.astype(jnp.float32) / length
    scale = 1.0 / math.sqrt(length)
    cos_part = (jnp.cos(angle) * scale).astype(jnp.float32)
    sin_part = (-jnp.sin(angle) * scale).astype(jnp.float32)
    neg_part = (jnp.sin(angle) * scale).astype(jnp.float32)
    right_fwd = jnp.concatenate([cos_part, sin_part], axis=1)
    left_fwd = jnp.concatenate([cos_part, sin_part], axis=0)
    right_inv = jnp.concatenate([cos_part, neg_part], axis=1)
    left_inv = jnp.concatenate([cos_part, neg_part], axis=0)
    freq = ((index_row + length // 2) % length - length // 2).astype(jnp.float32)
    phase = -math.pi * (freq[:, None] * freq[:, None] + freq[None, :] * freq[None, :]) / (2.0 * length)
    return (right_fwd, left_fwd, right_inv, left_inv, jnp.cos(phase), jnp.sin(phase))

def transform(real_in, imag_in, right_tab, left_tab):
    length = real_in.shape[0]
    stacked = jnp.concatenate([real_in, imag_in], axis=0)
    first_pass = jnp.dot(stacked, right_tab, precision=highest, preferred_element_type=jnp.float32)
    mid_real = first_pass[:length, :length] - first_pass[length:, length:]
    mid_imag = first_pass[:length, length:] + first_pass[length:, :length]
    second = jnp.dot(left_tab, jnp.concatenate([mid_real, mid_imag], axis=1), precision=highest, preferred_element_type=jnp.float32)
    out_real = second[:length, :length] - second[length:, length:]
    out_imag = second[:length, length:] + second[length:, :length]
    return (out_real, out_imag)

def transmit(wave_in, window):
    real_t = wave_in[0] * window[0] - wave_in[1] * window[1]
    imag_t = wave_in[0] * window[1] + wave_in[1] * window[0]
    return (real_t, imag_t)

def advance(wave_in, window, tables):
    right_fwd, left_fwd, right_inv, left_inv, prop_cos, prop_sin = tables
    real_t, imag_t = transmit(wave_in, window)
    spec_real, spec_imag = transform(real_t, imag_t, right_fwd, left_fwd)
    prop_real = spec_real * prop_cos - spec_imag * prop_sin
    prop_imag = spec_real * prop_sin + spec_imag * prop_cos
    out_real, out_imag = transform(prop_real, prop_imag, right_inv, left_inv)
    return jnp.stack([out_real, out_imag])

def exit_adjoint(wave_in, window, amplitude, tables):
    right_fwd, left_fwd = (tables[0], tables[1])
    real_t, imag_t = transmit(wave_in, window)
    far_real, far_imag = transform(real_t, imag_t, right_fwd, left_fwd)
    smooth = jnp.sqrt(far_real * far_real + far_imag * far_imag + smoothing)
    factor = 1.0 - amplitude.astype(jnp.float32) / smooth
    return jnp.stack([factor * far_real, factor * far_imag])

def unfold(adjoint, tables):
    out_real, out_imag = transform(adjoint[0], adjoint[1], tables[2], tables[3])
    return jnp.stack([out_real, out_imag])

def retreat(adjoint, tables):
    right_fwd, left_fwd, right_inv, left_inv, prop_cos, prop_sin = tables
    spec_real, spec_imag = transform(adjoint[0], adjoint[1], right_fwd, left_fwd)
    back_real = spec_real * prop_cos + spec_imag * prop_sin
    back_imag = spec_imag * prop_cos - spec_real * prop_sin
    out_real, out_imag = transform(back_real, back_imag, right_inv, left_inv)
    return jnp.stack([out_real, out_imag])

def slice_grad(wave_in, middle):
    return jnp.stack([wave_in[0] * middle[0] + wave_in[1] * middle[1], wave_in[0] * middle[1] - wave_in[1] * middle[0]])

def back_wave(window, middle):
    return jnp.stack([window[0] * middle[0] + window[1] * middle[1], window[0] * middle[1] - window[1] * middle[0]])

def reference(object_slices, probe_wave, amplitudes, positions, counts):
    tables = make_tables(WIN)
    total_rows = object_slices.shape[2]
    padded = jnp.concatenate([object_slices, object_slices[:, :, :WIN]], axis=2)
    zero_index = jnp.zeros((), jnp.int32)
    probe_float = probe_wave.astype(jnp.float32)

    def one_slot(gradient, slot_id):
        stripe_id = slot_id // CAP
        is_live = slot_id % CAP < counts[stripe_id]
        row_start = (stripe_id * STRIPE_ROWS + positions[slot_id, 0]).astype(jnp.int32)
        col_start = positions[slot_id, 1].astype(jnp.int32)
        corner = (zero_index, zero_index, row_start, col_start)

        def slot_work(gradient):
            windows = lax.dynamic_slice(padded, corner, (SLICES, 2, WIN, WIN))

            def forward_layer(wave_in, window):
                return (advance(wave_in, window, tables), wave_in)
            last_in, inputs = lax.scan(forward_layer, probe_float, windows[:-1])
            far_adj = exit_adjoint(last_in, windows[-1], amplitudes[slot_id], tables)
            middle = unfold(far_adj, tables)
            grad_last = slice_grad(last_in, middle)
            adjoint = back_wave(windows[-1], middle)

            def backward_layer(adjoint, pair_in):
                window, wave_in = pair_in
                middle = retreat(adjoint, tables)
                return (back_wave(window, middle), slice_grad(wave_in, middle))
            _, slice_grads = lax.scan(backward_layer, adjoint, (windows[:-1], inputs), reverse=True)
            all_grads = jnp.concatenate([slice_grads, grad_last[None]], axis=0)
            region = lax.dynamic_slice(gradient, corner, (SLICES, 2, WIN, WIN))
            return lax.dynamic_update_slice(gradient, region + all_grads, corner)
        return (lax.cond(is_live, slot_work, lambda kept: kept, gradient), None)
    start_grad = jnp.zeros(padded.shape, jnp.float32)
    gradient, _ = lax.scan(one_slot, start_grad, jnp.arange(SLOTS, dtype=jnp.int32))
    head_rows = gradient[:, :, :WIN] + gradient[:, :, total_rows:]
    return jnp.concatenate([head_rows, gradient[:, :, WIN:total_rows]], axis=2)
```

```python
import functools

import jax
import jax.numpy as jnp
import numpy as np
from jax import lax
from jax.experimental import pallas as pl
from jax.experimental.pallas import tpu as pltpu
from jax.sharding import PartitionSpec as P

smoothing = 0.25
LEVELS = 32767.0
MESH = pl.DeviceIdType.MESH


def right_form(matrix):
    return np.block([[matrix.real, matrix.imag], [-matrix.imag, matrix.real]])


def make_tables(length):
    half = length // 2
    index = np.arange(length)
    dft = np.exp(-2j * np.pi * (np.outer(index, index) % length) / length) / np.sqrt(length)
    freq = (index + half) % length - half
    fresnel = np.exp(-1j * np.pi * freq.astype(np.float64) ** 2 / (2.0 * length))
    prop = dft.conj() @ (fresnel[:, None] * dft)
    first, second = prop[:half, :half], prop[:half, half:]
    parts = [(first + second) / 2, (first - second) / 2, dft[:half, 0::2], dft[:half, 1::2]]
    tables = []
    for part in parts:
        right = right_form(part)
        tables += [right, right.T]
    stacked = np.stack(tables).astype(np.float32)
    high = stacked.astype(jnp.bfloat16)
    low = (stacked - high.astype(np.float32)).astype(jnp.bfloat16)
    order = np.concatenate([np.arange(0, length, 2), np.arange(1, length, 2)])
    pick = np.zeros((length, length), np.float32)
    pick[np.arange(length), order] = 1.0
    picks = np.stack([pick, pick.T]).astype(jnp.bfloat16)
    return np.concatenate([high, low, picks], axis=0)


def parts_of(value):
    high = value.astype(jnp.bfloat16)
    low = (value - high.astype(jnp.float32)).astype(jnp.bfloat16)
    return high, low


def dot(a, b):
    return jnp.dot(a, b, preferred_element_type=jnp.float32)


def worker_of(slot, stripe, stride):
    return slot * stride + lax.rem(slot + stripe, 2)


def kernel(
    depth_count, capacity, rows_ref, cols_ref, live_ref, win_ref, probe_ref, amp_ref, table_ref,
    own_ref, next_ref,
    wins, waves, gout, gscale, gin, gin_scale, rstack, lstack, adj_buf,
    send_w, recv_w, send_g, recv_g, send_s, recv_s,
):
    me = lax.axis_index("depth")
    stripe = lax.axis_index("stripe")
    stride = depth_count // capacity
    length = win_ref.shape[-1]
    half = length // 2
    count = (table_ref.shape[0] - 2) // 2

    barrier = pltpu.get_barrier_semaphore()

    @pl.loop(1, depth_count)
    def greet(step):
        other = lax.rem(me + step, depth_count)
        pl.semaphore_signal(barrier, inc=1, device_id=(other, stripe), device_id_type=MESH)

    pl.semaphore_wait(barrier, depth_count - 1)

    def window_copy(slot, target):
        return pltpu.make_async_remote_copy(
            src_ref=win_ref.at[slot], dst_ref=wins.at[me], send_sem=send_w.at[slot],
            recv_sem=recv_w.at[me], device_id=(target, stripe), device_id_type=MESH,
        )

    for slot in range(capacity):
        target = worker_of(slot, stripe, stride)

        @pl.when(me != target)
        def _():
            window_copy(slot, target).start()

        @pl.when(me == target)
        def _():
            pltpu.make_async_copy(win_ref.at[slot], wins.at[me], recv_w.at[me]).start()

    my_slot = me // stride
    is_worker = me == worker_of(my_slot, stripe, stride)

    def wait_window(layer):
        pltpu.make_async_copy(win_ref.at[0], wins.at[layer], recv_w.at[layer]).wait()

    def grad_copy(layer):
        return pltpu.make_async_remote_copy(
            src_ref=gout.at[layer], dst_ref=gin.at[my_slot], send_sem=send_g.at[layer],
            recv_sem=recv_g.at[my_slot], device_id=(layer, stripe), device_id_type=MESH,
        )

    def scale_copy(layer):
        return pltpu.make_async_remote_copy(
            src_ref=gscale.at[layer], dst_ref=gin_scale.at[my_slot], send_sem=send_s.at[layer],
            recv_sem=recv_s.at[my_slot], device_id=(layer, stripe), device_id_type=MESH,
        )

    def right_dot(value, which):
        high, low = parts_of(value)
        return dot(jnp.concatenate([high, high, low], axis=1), rstack[which])

    def left_dot(which, value):
        high, low = parts_of(value)
        return dot(lstack[which], jnp.concatenate([high, high, low], axis=0))

    def split_lanes(re, im):
        return (
            jnp.concatenate([re[:, :half] + re[:, half:], im[:, :half] + im[:, half:]], axis=1),
            jnp.concatenate([re[:, :half] - re[:, half:], im[:, :half] - im[:, half:]], axis=1),
        )

    def split_rows(re, im):
        return (
            jnp.concatenate([re[:half] + re[half:], im[:half] + im[half:]], axis=0),
            jnp.concatenate([re[:half] - re[half:], im[:half] - im[half:]], axis=0),
        )

    def join_lanes(p, q):
        return (
            jnp.concatenate([p[:, :half] + q[:, :half], p[:, :half] - q[:, :half]], axis=1),
            jnp.concatenate([p[:, half:] + q[:, half:], p[:, half:] - q[:, half:]], axis=1),
        )

    def join_rows(p, q):
        return (
            jnp.concatenate([p[:half] + q[:half], p[:half] - q[:half]], axis=0),
            jnp.concatenate([p[half:] + q[half:], p[half:] - q[half:]], axis=0),
        )

    def propagate(re, im):
        u, v = split_lanes(re, im)
        re, im = join_lanes(right_dot(u, 0), right_dot(v, 1))
        u, v = split_rows(re, im)
        return join_rows(left_dot(0, u), left_dot(1, v))

    def window_of(layer):
        value = wins[layer].astype(jnp.int32).astype(jnp.float32) * (1.0 / LEVELS)
        return value[0], value[1]

    def emit(layer, re, im):
        for part, value in enumerate((re, im)):
            most = jnp.max(jnp.abs(value), axis=0, keepdims=True)
            most = jnp.maximum(most, 1e-30)
            gout[layer, part] = jnp.round(value * (LEVELS / most)).astype(jnp.int32).astype(jnp.int16)
            gscale[layer, pl.ds(part, 1), :] = most * (1.0 / LEVELS)

        @pl.when(layer != me)
        def _():
            grad_copy(layer).start()
            scale_copy(layer).start()

        @pl.when(layer == me)
        def _():
            pltpu.make_async_copy(gout.at[layer], gin.at[my_slot], recv_g.at[my_slot]).start()
            pltpu.make_async_copy(gscale.at[layer], gin_scale.at[my_slot], recv_s.at[my_slot]).start()

    @pl.when(is_worker)
    def _():
        for which in range(count // 2):
            high, low = table_ref[2 * which], table_ref[count + 2 * which]
            rstack[which] = jnp.concatenate([high, low, high], axis=0)
            high, low = table_ref[2 * which + 1], table_ref[count + 2 * which + 1]
            lstack[which] = jnp.concatenate([high, low, high], axis=1)
        waves[0] = probe_ref[...].astype(jnp.float32)
        gscale[...] = jnp.zeros(gscale.shape, jnp.float32)

        @pl.loop(0, depth_count - 1)
        def forward(layer):
            wait_window(layer)
            win_re, win_im = window_of(layer)
            re, im = waves[layer, 0], waves[layer, 1]
            re, im = propagate(re * win_re - im * win_im, re * win_im + im * win_re)
            waves[layer + 1, 0] = re
            waves[layer + 1, 1] = im

        last = depth_count - 1
        wait_window(last)
        win_re, win_im = window_of(last)
        wave_re, wave_im = waves[last, 0], waves[last, 1]
        re = wave_re * win_re - wave_im * win_im
        im = wave_re * win_im + wave_im * win_re
        u, v = split_lanes(re, im)
        even, odd = right_dot(u, 2), right_dot(v, 3)
        re = jnp.concatenate([even[:, :half], odd[:, :half]], axis=1)
        im = jnp.concatenate([even[:, half:], odd[:, half:]], axis=1)
        u, v = split_rows(re, im)
        even, odd = left_dot(2, u), left_dot(3, v)
        pick_rows, pick_cols = table_ref[2 * count], table_ref[2 * count + 1]
        amp = dot(dot(pick_rows, amp_ref[...]).astype(jnp.bfloat16), pick_cols)
        re = jnp.concatenate([even[:half], odd[:half]], axis=0)
        im = jnp.concatenate([even[half:], odd[half:]], axis=0)
        factor = 1.0 - amp / jnp.sqrt(re * re + im * im + smoothing)
        re, im = factor * re, factor * im
        def left_back(which, value):
            high, low = parts_of(value)
            table = table_ref[2 * which]
            table_low = table_ref[count + 2 * which]
            return dot(table, high) + dot(table_low, high) + dot(table, low)

        def right_back(value, which):
            high, low = parts_of(value)
            table = table_ref[2 * which + 1]
            table_low = table_ref[count + 2 * which + 1]
            return dot(high, table) + dot(high, table_low) + dot(low, table)

        re, im = join_rows(
            left_back(2, jnp.concatenate([re[:half], im[:half]], axis=0)),
            left_back(3, jnp.concatenate([re[half:], im[half:]], axis=0)),
        )
        mid_re, mid_im = join_lanes(
            right_back(jnp.concatenate([re[:, :half], im[:, :half]], axis=1), 2),
            right_back(jnp.concatenate([re[:, half:], im[:, half:]], axis=1), 3),
        )
        emit(
            last,
            wave_re * mid_re + wave_im * mid_im,
            wave_re * mid_im - wave_im * mid_re,
        )
        adj_buf[0] = win_re * mid_re + win_im * mid_im
        adj_buf[1] = win_im * mid_re - win_re * mid_im

        @pl.loop(1, depth_count)
        def backward(step):
            layer = last - step
            mid_re, mid_conj = propagate(adj_buf[0], adj_buf[1])
            win_re, win_im = window_of(layer)
            wave_re, wave_im = waves[layer, 0], waves[layer, 1]
            emit(
                layer,
                wave_re * mid_re - wave_im * mid_conj,
                -(wave_re * mid_conj + wave_im * mid_re),
            )
            adj_buf[0] = win_re * mid_re - win_im * mid_conj
            adj_buf[1] = win_im * mid_re + win_re * mid_conj

    rows = own_ref.shape[1]
    row_index = lax.broadcasted_iota(jnp.int32, (rows, half), 0)
    col_index = lax.broadcasted_iota(jnp.int32, (rows, half), 1)
    own_ref[...] = jnp.zeros(own_ref.shape, jnp.float32)
    next_ref[...] = jnp.zeros(next_ref.shape, jnp.float32)
    for slot in range(capacity):
        pltpu.make_async_copy(gout.at[0], gin.at[slot], recv_g.at[slot]).wait()
        pltpu.make_async_copy(gscale.at[0], gin_scale.at[slot], recv_s.at[slot]).wait()
        row, col, live = rows_ref[slot], cols_ref[slot], live_ref[slot]
        here = row_index >= row
        near = col_index >= col
        for part in range(2):
            value = gin[slot, part].astype(jnp.int32).astype(jnp.float32)
            value = value * gin_scale[slot, pl.ds(part, 1), :]
            value = jnp.where(live > 0, value, 0.0)
            left, mid = value[:, :half], value[:, half:]
            pieces = (jnp.where(near, left, 0.0), mid, jnp.where(near, 0.0, left))
            for place, piece in enumerate(pieces):
                lanes = pl.ds(place * half, half)
                own_ref[part, :, lanes] += jnp.where(here, piece, 0.0)
                next_ref[part, :, lanes] += jnp.where(here, 0.0, piece)

    for slot in range(capacity):
        target = worker_of(slot, stripe, stride)

        @pl.when(me != target)
        def _():
            window_copy(slot, target).wait_send()

    @pl.when(is_worker)
    def _():
        @pl.loop(0, depth_count)
        def drain(layer):
            @pl.when(layer != me)
            def _():
                grad_copy(layer).wait_send()
                scale_copy(layer).wait_send()


def body(tables, object_slices, probe_wave, amplitudes, positions, counts):
    stripe = lax.axis_index("stripe")
    stripe_count = lax.axis_size("stripe")
    depth = lax.axis_index("depth")
    depth_count = lax.axis_size("depth")
    layers, _, stripe_rows, width = object_slices.shape
    length = probe_wave.shape[1]
    half = length // 2
    capacity = amplitudes.shape[0]
    stride = depth_count // capacity
    assert layers == 1 and stripe_rows == length and width == 3 * half and stride >= 2

    slab = jnp.round(object_slices[0] * LEVELS).astype(jnp.int16)
    back = [(i, (i + stripe_count - 1) % stripe_count) for i in range(stripe_count)]
    forth = [(i, (i + 1) % stripe_count) for i in range(stripe_count)]
    slab_next = lax.ppermute(slab, "stripe", back)

    mine = lax.dynamic_slice(positions, (stripe * capacity, 0), (capacity, 2)).astype(jnp.int32)
    rows, cols = mine[:, 0], mine[:, 1]
    live = (jnp.arange(capacity, dtype=jnp.int32) < counts[stripe]).astype(jnp.int32)
    here = jnp.arange(stripe_rows)[None, :] >= rows[:, None]
    near = jnp.arange(length)[None, :] >= cols[:, None]
    merged = jnp.where(here[:, None, :, None], slab[None], slab_next[None])
    folded = jnp.concatenate([merged[..., length:], merged[..., half:length]], axis=-1)
    windows = jnp.where(near[:, None, None, :], merged[..., :length], folded)

    my_slot = depth // stride
    row, col = rows[my_slot], cols[my_slot]
    doubled = jnp.concatenate([probe_wave, probe_wave], axis=1)
    probe = lax.dynamic_slice_in_dim(doubled, length - row, length, axis=1)
    doubled = jnp.concatenate([probe, probe], axis=2)
    probe = lax.dynamic_slice_in_dim(doubled, length - col, length, axis=2)
    amp = lax.dynamic_index_in_dim(amplitudes, my_slot, 0, keepdims=False)

    field = (2, length, length)
    vmem = pl.BlockSpec(memory_space=pltpu.VMEM)
    smem = pl.BlockSpec(memory_space=pltpu.SMEM)
    count = (tables.shape[0] - 2) // 4
    out = jax.ShapeDtypeStruct((2, stripe_rows, width), jnp.float32)
    own, following = pl.pallas_call(
        functools.partial(kernel, depth_count, capacity),
        out_shape=(out, out),
        in_specs=[smem] * 3 + [vmem] * 4,
        out_specs=(vmem, vmem),
        scratch_shapes=[
            pltpu.VMEM((depth_count,) + field, jnp.int16),
            pltpu.VMEM((depth_count,) + field, jnp.float32),
            pltpu.VMEM((depth_count,) + field, jnp.int16),
            pltpu.VMEM((depth_count, 8, length), jnp.float32),
            pltpu.VMEM((capacity,) + field, jnp.int16),
            pltpu.VMEM((capacity, 8, length), jnp.float32),
            pltpu.VMEM((count, 3 * length, length), jnp.bfloat16),
            pltpu.VMEM((count, length, 3 * length), jnp.bfloat16),
            pltpu.VMEM(field, jnp.float32),
            pltpu.SemaphoreType.DMA((capacity,)),
            pltpu.SemaphoreType.DMA((depth_count,)),
            pltpu.SemaphoreType.DMA((depth_count,)),
            pltpu.SemaphoreType.DMA((capacity,)),
            pltpu.SemaphoreType.DMA((depth_count,)),
            pltpu.SemaphoreType.DMA((capacity,)),
        ],
        compiler_params=pltpu.CompilerParams(
            collective_id=0, has_side_effects=True, vmem_limit_bytes=60 * 1024 * 1024
        ),
    )(rows, cols, live, windows, probe, amp, tables)
    received = lax.ppermute(following, "stripe", forth)
    return (own + received)[None]


def solution(mesh):
    def run(object_slices, probe_wave, amplitudes, positions, counts):
        tables = jnp.asarray(make_tables(probe_wave.shape[1]))
        return jax.shard_map(
            body,
            mesh=mesh,
            in_specs=(P(), P("depth", None, "stripe", None), P(), P("stripe", None, None), P(), P()),
            out_specs=P("depth", None, "stripe", None),
            check_vma=False,
        )(tables, object_slices, probe_wave, amplitudes, positions, counts)

    return run
```

```python
import functools

import jax
import jax.numpy as jnp
import numpy as np
from jax import lax
from jax.experimental import pallas as pl
from jax.experimental.pallas import tpu as pltpu
from jax.sharding import PartitionSpec as P

smoothing = 0.25
LEVELS = 32767.0
MESH = pl.DeviceIdType.MESH


def right_form(matrix):
    return np.block([[matrix.real, matrix.imag], [-matrix.imag, matrix.real]])


def make_tables(length):
    half = length // 2
    index = np.arange(length)
    dft = np.exp(-2j * np.pi * (np.outer(index, index) % length) / length) / np.sqrt(length)
    freq = (index + half) % length - half
    fresnel = np.exp(-1j * np.pi * freq.astype(np.float64) ** 2 / (2.0 * length))
    prop = dft.conj() @ (fresnel[:, None] * dft)
    first, second = prop[:half, :half], prop[:half, half:]
    parts = [(first + second) / 2, (first - second) / 2, dft[:half, 0::2], dft[:half, 1::2]]
    tables = []
    for part in parts:
        right = right_form(part)
        tables += [right, right.T]
    stacked = np.stack(tables).astype(np.float32)
    high = stacked.astype(jnp.bfloat16)
    low = (stacked - high.astype(np.float32)).astype(jnp.bfloat16)
    order = np.concatenate([np.arange(0, length, 2), np.arange(1, length, 2)])
    pick = np.zeros((length, length), np.float32)
    pick[np.arange(length), order] = 1.0
    picks = np.stack([pick, pick.T]).astype(jnp.bfloat16)
    return np.concatenate([high, low, picks], axis=0)


def parts_of(value):
    high = value.astype(jnp.bfloat16)
    low = (value - high.astype(jnp.float32)).astype(jnp.bfloat16)
    return high, low


def dot(a, b):
    return jnp.dot(a, b, preferred_element_type=jnp.float32)


def kernel(
    depth_count, stripe_count, capacity, positions_ref, counts_ref, object_ref, probe_ref, amp_ref,
    table_ref, out_ref,
    slab, slab_next, win, wins, waves, gout, gscale, gin, gin_scale, rstack, lstack, adj_buf,
    following, following_scale, given, given_scale,
    send_n, recv_n, send_w, recv_w, send_g, recv_g, send_s, recv_s, send_f, recv_f, send_fs, recv_fs,
):
    me = lax.axis_index("depth")
    stripe = lax.axis_index("stripe")
    stride = depth_count // capacity
    length = probe_ref.shape[-1]
    half = length // 2
    count = (table_ref.shape[0] - 2) // 2
    before = lax.rem(stripe + stripe_count - 1, stripe_count)
    after = lax.rem(stripe + 1, stripe_count)

    barrier = pltpu.get_barrier_semaphore()

    @pl.loop(1, depth_count)
    def greet(step):
        other = lax.rem(me + step, depth_count)
        pl.semaphore_signal(barrier, inc=1, device_id=(other, stripe), device_id_type=MESH)

    pl.semaphore_signal(barrier, inc=1, device_id=(me, before), device_id_type=MESH)
    pl.semaphore_signal(barrier, inc=1, device_id=(me, after), device_id_type=MESH)
    for part in range(2):
        slab[part] = jnp.round(object_ref[0, part] * LEVELS).astype(jnp.int32).astype(jnp.int16)
    pl.semaphore_wait(barrier, depth_count + 1)

    def slab_copy(part):
        return pltpu.make_async_remote_copy(
            src_ref=slab.at[part], dst_ref=slab_next.at[part], send_sem=send_n.at[part],
            recv_sem=recv_n.at[part], device_id=(me, before), device_id_type=MESH,
        )

    for part in range(2):
        slab_copy(part).start()

    def worker_of(slot):
        return slot * stride + lax.rem(slot + stripe, 2)

    my_slot = me // stride
    is_worker = me == worker_of(my_slot)

    @pl.when(is_worker)
    def _():
        for which in range(count // 2):
            high, low = table_ref[2 * which], table_ref[count + 2 * which]
            rstack[which] = jnp.concatenate([high, low, high], axis=0)
            high, low = table_ref[2 * which + 1], table_ref[count + 2 * which + 1]
            lstack[which] = jnp.concatenate([high, low, high], axis=1)
        gscale[...] = jnp.zeros(gscale.shape, jnp.float32)
        row = positions_ref[stripe * capacity + my_slot, 0]
        col = positions_ref[stripe * capacity + my_slot, 1]
        first = lax.broadcasted_iota(jnp.int32, (length, length), 0)
        second = lax.broadcasted_iota(jnp.int32, (length, length), 1)
        turned = second + row
        turned = jnp.where(turned >= length, turned - length, turned)
        turn_rows = jnp.where(first == turned, 1.0, 0.0).astype(jnp.bfloat16)
        turned = first + col
        turned = jnp.where(turned >= length, turned - length, turned)
        turn_cols = jnp.where(second == turned, 1.0, 0.0).astype(jnp.bfloat16)
        for part in range(2):
            value = dot(turn_rows, probe_ref[part]).astype(jnp.bfloat16)
            waves[0, part] = dot(value, turn_cols)

    def window_copy(slot, part, target):
        return pltpu.make_async_remote_copy(
            src_ref=win.at[slot, part], dst_ref=wins.at[me, part], send_sem=send_w.at[slot, part],
            recv_sem=recv_w.at[me, part], device_id=(target, stripe), device_id_type=MESH,
        )

    row_index = lax.broadcasted_iota(jnp.int32, (length, half), 0)
    col_index = lax.broadcasted_iota(jnp.int32, (length, half), 1)
    for part in range(2):
        slab_copy(part).wait_recv()
        for slot in range(capacity):
            row = positions_ref[stripe * capacity + slot, 0]
            col = positions_ref[stripe * capacity + slot, 1]
            here = row_index >= row
            near = col_index >= col
            left, mid, right = (
                jnp.where(
                    here,
                    slab[part, :, pl.ds(place * half, half)].astype(jnp.int32),
                    slab_next[part, :, pl.ds(place * half, half)].astype(jnp.int32),
                )
                for place in range(3)
            )
            win[slot, part, :, pl.ds(0, half)] = jnp.where(near, left, right).astype(jnp.int16)
            win[slot, part, :, pl.ds(half, half)] = mid.astype(jnp.int16)
            target = worker_of(slot)

            @pl.when(me != target)
            def _():
                window_copy(slot, part, target).start()

            @pl.when(me == target)
            def _():
                pltpu.make_async_copy(
                    win.at[slot, part], wins.at[me, part], recv_w.at[me, part]
                ).start()

    def wait_window(layer):
        for part in range(2):
            pltpu.make_async_copy(
                win.at[0, part], wins.at[layer, part], recv_w.at[layer, part]
            ).wait()

    def grad_copy(layer):
        return pltpu.make_async_remote_copy(
            src_ref=gout.at[layer], dst_ref=gin.at[my_slot], send_sem=send_g.at[layer],
            recv_sem=recv_g.at[my_slot], device_id=(layer, stripe), device_id_type=MESH,
        )

    def scale_copy(layer):
        return pltpu.make_async_remote_copy(
            src_ref=gscale.at[layer], dst_ref=gin_scale.at[my_slot], send_sem=send_s.at[layer],
            recv_sem=recv_s.at[my_slot], device_id=(layer, stripe), device_id_type=MESH,
        )

    def right_dot(value, which):
        high, low = parts_of(value)
        return dot(jnp.concatenate([high, high, low], axis=1), rstack[which])

    def left_dot(which, value):
        high, low = parts_of(value)
        return dot(lstack[which], jnp.concatenate([high, high, low], axis=0))

    def split_lanes(re, im):
        return (
            jnp.concatenate([re[:, :half] + re[:, half:], im[:, :half] + im[:, half:]], axis=1),
            jnp.concatenate([re[:, :half] - re[:, half:], im[:, :half] - im[:, half:]], axis=1),
        )

    def split_rows(re, im):
        return (
            jnp.concatenate([re[:half] + re[half:], im[:half] + im[half:]], axis=0),
            jnp.concatenate([re[:half] - re[half:], im[:half] - im[half:]], axis=0),
        )

    def join_lanes(p, q):
        return (
            jnp.concatenate([p[:, :half] + q[:, :half], p[:, :half] - q[:, :half]], axis=1),
            jnp.concatenate([p[:, half:] + q[:, half:], p[:, half:] - q[:, half:]], axis=1),
        )

    def join_rows(p, q):
        return (
            jnp.concatenate([p[:half] + q[:half], p[:half] - q[:half]], axis=0),
            jnp.concatenate([p[half:] + q[half:], p[half:] - q[half:]], axis=0),
        )

    def propagate(re, im):
        u, v = split_lanes(re, im)
        re, im = join_lanes(right_dot(u, 0), right_dot(v, 1))
        u, v = split_rows(re, im)
        return join_rows(left_dot(0, u), left_dot(1, v))

    def window_of(layer):
        value = wins[layer].astype(jnp.int32).astype(jnp.float32) * (1.0 / LEVELS)
        return value[0], value[1]

    def emit(layer, re, im):
        for part, value in enumerate((re, im)):
            most = jnp.max(jnp.abs(value), axis=0, keepdims=True)
            most = jnp.maximum(most, 1e-30)
            gout[layer, part] = jnp.round(value * (LEVELS / most)).astype(jnp.int32).astype(jnp.int16)
            gscale[layer, pl.ds(part, 1), :] = most * (1.0 / LEVELS)

        @pl.when(layer != me)
        def _():
            grad_copy(layer).start()
            scale_copy(layer).start()

        @pl.when(layer == me)
        def _():
            pltpu.make_async_copy(gout.at[layer], gin.at[my_slot], recv_g.at[my_slot]).start()
            pltpu.make_async_copy(gscale.at[layer], gin_scale.at[my_slot], recv_s.at[my_slot]).start()

    @pl.when(is_worker)
    def _():
        @pl.loop(0, depth_count - 1)
        def forward(layer):
            wait_window(layer)
            win_re, win_im = window_of(layer)
            re, im = waves[layer, 0], waves[layer, 1]
            re, im = propagate(re * win_re - im * win_im, re * win_im + im * win_re)
            waves[layer + 1, 0] = re
            waves[layer + 1, 1] = im

        last = depth_count - 1
        wait_window(last)
        win_re, win_im = window_of(last)
        wave_re, wave_im = waves[last, 0], waves[last, 1]
        re = wave_re * win_re - wave_im * win_im
        im = wave_re * win_im + wave_im * win_re
        u, v = split_lanes(re, im)
        even, odd = right_dot(u, 2), right_dot(v, 3)
        re = jnp.concatenate([even[:, :half], odd[:, :half]], axis=1)
        im = jnp.concatenate([even[:, half:], odd[:, half:]], axis=1)
        u, v = split_rows(re, im)
        even, odd = left_dot(2, u), left_dot(3, v)
        pick_rows, pick_cols = table_ref[2 * count], table_ref[2 * count + 1]
        amp = dot(dot(pick_rows, amp_ref[my_slot]).astype(jnp.bfloat16), pick_cols)
        re = jnp.concatenate([even[:half], odd[:half]], axis=0)
        im = jnp.concatenate([even[half:], odd[half:]], axis=0)
        factor = 1.0 - amp / jnp.sqrt(re * re + im * im + smoothing)
        re, im = factor * re, factor * im
        def left_back(which, value):
            high, low = parts_of(value)
            table = table_ref[2 * which]
            table_low = table_ref[count + 2 * which]
            return dot(table, high) + dot(table_low, high) + dot(table, low)

        def right_back(value, which):
            high, low = parts_of(value)
            table = table_ref[2 * which + 1]
            table_low = table_ref[count + 2 * which + 1]
            return dot(high, table) + dot(high, table_low) + dot(low, table)

        re, im = join_rows(
            left_back(2, jnp.concatenate([re[:half], im[:half]], axis=0)),
            left_back(3, jnp.concatenate([re[half:], im[half:]], axis=0)),
        )
        mid_re, mid_im = join_lanes(
            right_back(jnp.concatenate([re[:, :half], im[:, :half]], axis=1), 2),
            right_back(jnp.concatenate([re[:, half:], im[:, half:]], axis=1), 3),
        )
        emit(
            last,
            wave_re * mid_re + wave_im * mid_im,
            wave_re * mid_im - wave_im * mid_re,
        )
        adj_buf[0] = win_re * mid_re + win_im * mid_im
        adj_buf[1] = win_im * mid_re - win_re * mid_im

        @pl.loop(1, depth_count)
        def backward(step):
            layer = last - step
            mid_re, mid_conj = propagate(adj_buf[0], adj_buf[1])
            win_re, win_im = window_of(layer)
            wave_re, wave_im = waves[layer, 0], waves[layer, 1]
            emit(
                layer,
                wave_re * mid_re - wave_im * mid_conj,
                -(wave_re * mid_conj + wave_im * mid_re),
            )
            adj_buf[0] = win_re * mid_re - win_im * mid_conj
            adj_buf[1] = win_im * mid_re + win_re * mid_conj

    def following_copy(part):
        return pltpu.make_async_remote_copy(
            src_ref=following.at[part], dst_ref=given.at[part], send_sem=send_f.at[part],
            recv_sem=recv_f.at[part], device_id=(me, after), device_id_type=MESH,
        )

    def following_scale_copy(part):
        return pltpu.make_async_remote_copy(
            src_ref=following_scale.at[part], dst_ref=given_scale.at[part],
            send_sem=send_fs.at[part], recv_sem=recv_fs.at[part], device_id=(me, after),
            device_id_type=MESH,
        )

    following_scale[...] = jnp.zeros(following_scale.shape, jnp.float32)
    for slot in range(capacity):
        pltpu.make_async_copy(gout.at[0], gin.at[slot], recv_g.at[slot]).wait()
        pltpu.make_async_copy(gscale.at[0], gin_scale.at[slot], recv_s.at[slot]).wait()
    for part in range(2):
        own_sums, next_sums = [0.0] * 3, [0.0] * 3
        for slot in range(capacity):
            row = positions_ref[stripe * capacity + slot, 0]
            col = positions_ref[stripe * capacity + slot, 1]
            here = row_index >= row
            near = col_index >= col
            live = counts_ref[stripe] > slot
            scale = gin_scale[slot, pl.ds(part, 1), :]
            scale = jnp.where(live, scale, 0.0)
            left = gin[slot, part, :, pl.ds(0, half)].astype(jnp.int32).astype(jnp.float32)
            left = left * scale[:, :half]
            mid = gin[slot, part, :, pl.ds(half, half)].astype(jnp.int32).astype(jnp.float32)
            mid = mid * scale[:, half:]
            pieces = (jnp.where(near, left, 0.0), mid, jnp.where(near, 0.0, left))
            for place, piece in enumerate(pieces):
                own_sums[place] = own_sums[place] + jnp.where(here, piece, 0.0)
                next_sums[place] = next_sums[place] + jnp.where(here, 0.0, piece)
        for place in range(3):
            lanes = pl.ds(place * half, half)
            most = jnp.max(jnp.abs(next_sums[place]), axis=0, keepdims=True)
            most = jnp.maximum(most, 1e-30)
            whole = jnp.round(next_sums[place] * (LEVELS / most)).astype(jnp.int32)
            following[part, :, lanes] = whole.astype(jnp.int16)
            following_scale[part, pl.ds(0, 1), lanes] = most * (1.0 / LEVELS)
            out_ref[0, part, :, lanes] = own_sums[place]
        following_copy(part).start()
        following_scale_copy(part).start()

    for part in range(2):
        following_copy(part).wait_recv()
        following_scale_copy(part).wait_recv()
        value = given[part].astype(jnp.int32).astype(jnp.float32)
        out_ref[0, part] += value * given_scale[part, pl.ds(0, 1), :]

    for part in range(2):
        slab_copy(part).wait_send()
        following_copy(part).wait_send()
        following_scale_copy(part).wait_send()
    for slot in range(capacity):
        target = worker_of(slot)

        @pl.when(me != target)
        def _():
            for part in range(2):
                window_copy(slot, part, target).wait_send()

    @pl.when(is_worker)
    def _():
        @pl.loop(0, depth_count)
        def drain(layer):
            @pl.when(layer != me)
            def _():
                grad_copy(layer).wait_send()
                scale_copy(layer).wait_send()


def body(tables, object_slices, probe_wave, amplitudes, positions, counts):
    stripe_count = lax.axis_size("stripe")
    depth_count = lax.axis_size("depth")
    layers, _, stripe_rows, width = object_slices.shape
    length = probe_wave.shape[1]
    capacity = amplitudes.shape[0]
    assert layers == 1 and stripe_rows == length and 2 * width == 3 * length
    assert depth_count >= 2 * capacity and stripe_count > 2

    field = (2, length, length)
    slab = (2, stripe_rows, width)
    slab_scale = (2, 8, width)
    vmem = pl.BlockSpec(memory_space=pltpu.VMEM)
    smem = pl.BlockSpec(memory_space=pltpu.SMEM)
    dma = pltpu.SemaphoreType.DMA
    count = (tables.shape[0] - 2) // 4
    return pl.pallas_call(
        functools.partial(kernel, depth_count, stripe_count, capacity),
        out_shape=jax.ShapeDtypeStruct(object_slices.shape, jnp.float32),
        in_specs=[smem] * 2 + [vmem] * 4,
        out_specs=vmem,
        scratch_shapes=[
            pltpu.VMEM(slab, jnp.int16),
            pltpu.VMEM(slab, jnp.int16),
            pltpu.VMEM((capacity,) + field, jnp.int16),
            pltpu.VMEM((depth_count,) + field, jnp.int16),
            pltpu.VMEM((depth_count,) + field, jnp.float32),
            pltpu.VMEM((depth_count,) + field, jnp.int16),
            pltpu.VMEM((depth_count, 8, length), jnp.float32),
            pltpu.VMEM((capacity,) + field, jnp.int16),
            pltpu.VMEM((capacity, 8, length), jnp.float32),
            pltpu.VMEM((count, 3 * length, length), jnp.bfloat16),
            pltpu.VMEM((count, length, 3 * length), jnp.bfloat16),
            pltpu.VMEM(field, jnp.float32),
            pltpu.VMEM(slab, jnp.int16),
            pltpu.VMEM(slab_scale, jnp.float32),
            pltpu.VMEM(slab, jnp.int16),
            pltpu.VMEM(slab_scale, jnp.float32),
            dma((2,)),
            dma((2,)),
            dma((capacity, 2)),
            dma((depth_count, 2)),
            dma((depth_count,)),
            dma((capacity,)),
            dma((depth_count,)),
            dma((capacity,)),
            dma((2,)),
            dma((2,)),
            dma((2,)),
            dma((2,)),
        ],
        compiler_params=pltpu.CompilerParams(
            collective_id=0, has_side_effects=True, vmem_limit_bytes=60 * 1024 * 1024
        ),
    )(positions, counts, object_slices, probe_wave, amplitudes, tables)


def solution(mesh):
    def run(object_slices, probe_wave, amplitudes, positions, counts):
        tables = jnp.asarray(make_tables(probe_wave.shape[1]))
        return jax.shard_map(
            body,
            mesh=mesh,
            in_specs=(P(), P("depth", None, "stripe", None), P(), P("stripe", None, None), P(), P()),
            out_specs=P("depth", None, "stripe", None),
            check_vma=False,
        )(tables, object_slices, probe_wave, amplitudes, positions, counts)

    return run
```

```python
import functools

import jax
import jax.numpy as jnp
import numpy as np
from jax import lax
from jax.experimental import pallas as pl
from jax.experimental.pallas import tpu as pltpu
from jax.sharding import PartitionSpec as P

smoothing = 0.25
LEVELS = 32767.0
MESH = pl.DeviceIdType.MESH


def right_form(matrix):
    return np.block([[matrix.real, matrix.imag], [-matrix.imag, matrix.real]])


def make_tables(length):
    half = length // 2
    index = np.arange(length)
    dft = np.exp(-2j * np.pi * (np.outer(index, index) % length) / length) / np.sqrt(length)
    freq = (index + half) % length - half
    fresnel = np.exp(-1j * np.pi * freq.astype(np.float64) ** 2 / (2.0 * length))
    prop = dft.conj() @ (fresnel[:, None] * dft)
    first, second = prop[:half, :half], prop[:half, half:]
    parts = [(first + second) / 2, (first - second) / 2, dft[:half, 0::2], dft[:half, 1::2]]
    tables = []
    for part in parts:
        right = right_form(part)
        tables += [right, right.T]
    stacked = np.stack(tables).astype(np.float32)
    high = stacked.astype(jnp.bfloat16)
    low = (stacked - high.astype(np.float32)).astype(jnp.bfloat16)
    order = np.concatenate([np.arange(0, length, 2), np.arange(1, length, 2)])
    pick = np.zeros((length, length), np.float32)
    pick[np.arange(length), order] = 1.0
    picks = np.stack([pick, pick.T]).astype(jnp.bfloat16)
    return np.concatenate([high, low, picks], axis=0)


def parts_of(value):
    high = value.astype(jnp.bfloat16)
    low = (value - high.astype(jnp.float32)).astype(jnp.bfloat16)
    return high, low


def dot(a, b):
    return jnp.dot(a, b, preferred_element_type=jnp.float32)


def kernel(
    depth_count, stripe_count, capacity, positions_ref, counts_ref, object_ref, probe_ref, amp_ref,
    table_ref, out_ref,
    slab_re, slab_im, win, wins, waves, gout, gscale, gin, gin_scale, rstack, lstack, adj_buf,
    patterns, across, across_scale, given, given_scale,
    send_n, recv_n, send_w, recv_w, send_g, recv_g, send_s, recv_s, send_h, send_hs, send_a, recv_a,
    send_f, recv_f, send_fs, recv_fs,
):
    me = lax.axis_index("depth")
    stripe = lax.axis_index("stripe")
    share = capacity // 2
    stride = depth_count // (share + 2)
    slabs = (slab_re, slab_im)
    length = probe_ref.shape[-1]
    half = length // 2
    count = (table_ref.shape[0] - 2) // 2
    partner = stripe + 1 - 2 * lax.rem(stripe, 2)
    opposite = lax.rem(stripe + 2, stripe_count)

    def slot_of(place):
        owner, passed, start = jnp.int32(0), jnp.int32(0), jnp.int32(0)
        for other in range(1, stripe_count):
            passed = passed + counts_ref[other - 1]
            owner = owner + jnp.where(place >= passed, 1, 0)
            start = jnp.where(place >= passed, passed, start)
        within = jnp.clip(place - start, 0, capacity - 1)
        slot = owner * capacity + within
        return owner, within, positions_ref[slot, 0], positions_ref[slot, 1]

    barrier = pltpu.get_barrier_semaphore()

    @pl.loop(1, depth_count)
    def greet(step):
        other = lax.rem(me + step, depth_count)
        pl.semaphore_signal(barrier, inc=1, device_id=(other, stripe), device_id_type=MESH)

    for step in range(1, stripe_count):
        other = lax.rem(stripe + step, stripe_count)
        pl.semaphore_signal(barrier, inc=1, device_id=(me, other), device_id_type=MESH)
    for part in range(2):
        whole = jnp.round(object_ref[0, part] * LEVELS).astype(jnp.int32)
        slabs[part][stripe] = whole.astype(jnp.int16)
    pl.semaphore_wait(barrier, depth_count + stripe_count - 2)

    def slab_copy(route, part):
        source = opposite if route == 2 else stripe
        target = opposite if route == 1 else partner
        return pltpu.make_async_remote_copy(
            src_ref=slabs[part].at[source], dst_ref=slabs[part].at[source],
            send_sem=send_n.at[route, part], recv_sem=recv_n.at[route, part],
            device_id=(me, target), device_id_type=MESH,
        )

    for part in range(2):
        slab_copy(1, part).start()
        slab_copy(0, part).start()

    def worker_of(slot):
        return (slot + 1) * stride + lax.rem(stripe, 2)

    base = jnp.maximum(me - lax.rem(stripe, 2), 0)
    my_slot = jnp.clip(base // stride - 1, 0, share - 1)
    is_worker = me == worker_of(my_slot)
    my_owner, my_within, my_row, my_col = slot_of(stripe * share + my_slot)

    def pattern_copy(parity, turn):
        return pltpu.make_async_remote_copy(
            src_ref=amp_ref, dst_ref=patterns.at[stripe], send_sem=send_a.at[turn],
            recv_sem=recv_a.at[stripe], device_id=(me, 2 * turn + parity), device_id_type=MESH,
        )

    def each_pattern_target(action):
        for parity in range(2):
            for slot in range(share):
                for turn in range(stripe_count // 2):
                    here = (me == (slot + 1) * stride + parity) & (stripe != 2 * turn + parity)

                    @pl.when(here)
                    def _():
                        action(pattern_copy(parity, turn))

    each_pattern_target(lambda copy: copy.start())

    for part in range(2):
        slab_copy(1, part).wait_recv()
        slab_copy(2, part).start()

    @pl.when(is_worker)
    def _():
        for which in range(count // 2):
            high, low = table_ref[2 * which], table_ref[count + 2 * which]
            rstack[which] = jnp.concatenate([high, low, high], axis=0)
            high, low = table_ref[2 * which + 1], table_ref[count + 2 * which + 1]
            lstack[which] = jnp.concatenate([high, low, high], axis=1)
        gscale[...] = jnp.zeros(gscale.shape, jnp.float32)
        pltpu.make_async_copy(amp_ref, patterns.at[stripe], recv_a.at[stripe]).start()
        first = lax.broadcasted_iota(jnp.int32, (length, length), 0)
        second = lax.broadcasted_iota(jnp.int32, (length, length), 1)
        turned = second + my_row
        turned = jnp.where(turned >= length, turned - length, turned)
        turn_rows = jnp.where(first == turned, 1.0, 0.0).astype(jnp.bfloat16)
        turned = first + my_col
        turned = jnp.where(turned >= length, turned - length, turned)
        turn_cols = jnp.where(second == turned, 1.0, 0.0).astype(jnp.bfloat16)
        for part in range(2):
            value = dot(turn_rows, probe_ref[part]).astype(jnp.bfloat16)
            waves[0, part] = dot(value, turn_cols)

    def window_copy(slot, part, target):
        return pltpu.make_async_remote_copy(
            src_ref=win.at[slot, part], dst_ref=wins.at[me, part], send_sem=send_w.at[slot, part],
            recv_sem=recv_w.at[me, part], device_id=(target, stripe), device_id_type=MESH,
        )

    row_index = lax.broadcasted_iota(jnp.int32, (length, half), 0)
    col_index = lax.broadcasted_iota(jnp.int32, (length, half), 1)
    for part in range(2):
        slab_copy(0, part).wait_recv()
        slab_copy(2, part).wait_recv()
        for slot in range(share):
            owner, _, row, col = slot_of(stripe * share + slot)
            later = lax.rem(owner + 1, stripe_count)
            here = row_index >= row
            near = col_index >= col
            left, mid, right = (
                jnp.where(
                    here,
                    slabs[part][owner, :, pl.ds(place * half, half)].astype(jnp.int32),
                    slabs[part][later, :, pl.ds(place * half, half)].astype(jnp.int32),
                )
                for place in range(3)
            )
            win[slot, part, :, pl.ds(0, half)] = jnp.where(near, left, right).astype(jnp.int16)
            win[slot, part, :, pl.ds(half, half)] = mid.astype(jnp.int16)
            target = worker_of(slot)

            @pl.when(me != target)
            def _():
                window_copy(slot, part, target).start()

            @pl.when(me == target)
            def _():
                pltpu.make_async_copy(
                    win.at[slot, part], wins.at[me, part], recv_w.at[me, part]
                ).start()

    def wait_window(layer):
        for part in range(2):
            pltpu.make_async_copy(
                win.at[0, part], wins.at[layer, part], recv_w.at[layer, part]
            ).wait()

    def grad_copy(layer):
        return pltpu.make_async_remote_copy(
            src_ref=gout.at[layer], dst_ref=gin.at[my_slot], send_sem=send_g.at[layer],
            recv_sem=recv_g.at[my_slot], device_id=(layer, stripe), device_id_type=MESH,
        )

    def scale_copy(layer):
        return pltpu.make_async_remote_copy(
            src_ref=gscale.at[layer], dst_ref=gin_scale.at[my_slot], send_sem=send_s.at[layer],
            recv_sem=recv_s.at[my_slot], device_id=(layer, stripe), device_id_type=MESH,
        )

    def right_dot(value, which):
        high, low = parts_of(value)
        return dot(jnp.concatenate([high, high, low], axis=1), rstack[which])

    def left_dot(which, value):
        high, low = parts_of(value)
        return dot(lstack[which], jnp.concatenate([high, high, low], axis=0))

    def split_lanes(re, im):
        return (
            jnp.concatenate([re[:, :half] + re[:, half:], im[:, :half] + im[:, half:]], axis=1),
            jnp.concatenate([re[:, :half] - re[:, half:], im[:, :half] - im[:, half:]], axis=1),
        )

    def split_rows(re, im):
        return (
            jnp.concatenate([re[:half] + re[half:], im[:half] + im[half:]], axis=0),
            jnp.concatenate([re[:half] - re[half:], im[:half] - im[half:]], axis=0),
        )

    def join_lanes(p, q):
        return (
            jnp.concatenate([p[:, :half] + q[:, :half], p[:, :half] - q[:, :half]], axis=1),
            jnp.concatenate([p[:, half:] + q[:, half:], p[:, half:] - q[:, half:]], axis=1),
        )

    def join_rows(p, q):
        return (
            jnp.concatenate([p[:half] + q[:half], p[:half] - q[:half]], axis=0),
            jnp.concatenate([p[half:] + q[half:], p[half:] - q[half:]], axis=0),
        )

    def propagate(re, im):
        u, v = split_lanes(re, im)
        re, im = join_lanes(right_dot(u, 0), right_dot(v, 1))
        u, v = split_rows(re, im)
        return join_rows(left_dot(0, u), left_dot(1, v))

    def window_of(layer):
        value = wins[layer].astype(jnp.int32).astype(jnp.float32) * (1.0 / LEVELS)
        return value[0], value[1]

    def emit(layer, re, im):
        for part, value in enumerate((re, im)):
            most = jnp.max(jnp.abs(value), axis=0, keepdims=True)
            most = jnp.maximum(most, 1e-30)
            gout[layer, part] = jnp.round(value * (LEVELS / most)).astype(jnp.int32).astype(jnp.int16)
            gscale[layer, pl.ds(part, 1), :] = most * (1.0 / LEVELS)

        @pl.when(layer != me)
        def _():
            grad_copy(layer).start()
            scale_copy(layer).start()

        @pl.when(layer == me)
        def _():
            pltpu.make_async_copy(gout.at[layer], gin.at[my_slot], recv_g.at[my_slot]).start()
            pltpu.make_async_copy(gscale.at[layer], gin_scale.at[my_slot], recv_s.at[my_slot]).start()

    @pl.when(is_worker)
    def _():
        @pl.loop(0, depth_count - 1)
        def forward(layer):
            wait_window(layer)
            win_re, win_im = window_of(layer)
            re, im = waves[layer, 0], waves[layer, 1]
            re, im = propagate(re * win_re - im * win_im, re * win_im + im * win_re)
            waves[layer + 1, 0] = re
            waves[layer + 1, 1] = im

        last = depth_count - 1
        wait_window(last)
        win_re, win_im = window_of(last)
        wave_re, wave_im = waves[last, 0], waves[last, 1]
        re = wave_re * win_re - wave_im * win_im
        im = wave_re * win_im + wave_im * win_re
        u, v = split_lanes(re, im)
        even, odd = right_dot(u, 2), right_dot(v, 3)
        re = jnp.concatenate([even[:, :half], odd[:, :half]], axis=1)
        im = jnp.concatenate([even[:, half:], odd[:, half:]], axis=1)
        u, v = split_rows(re, im)
        even, odd = left_dot(2, u), left_dot(3, v)
        for source in range(stripe_count):
            pltpu.make_async_copy(amp_ref, patterns.at[source], recv_a.at[source]).wait()
        pick_rows, pick_cols = table_ref[2 * count], table_ref[2 * count + 1]
        amp = dot(dot(pick_rows, patterns[my_owner, my_within]).astype(jnp.bfloat16), pick_cols)
        re = jnp.concatenate([even[:half], odd[:half]], axis=0)
        im = jnp.concatenate([even[half:], odd[half:]], axis=0)
        factor = 1.0 - amp / jnp.sqrt(re * re + im * im + smoothing)
        re, im = factor * re, factor * im
        def left_back(which, value):
            high, low = parts_of(value)
            table = table_ref[2 * which]
            table_low = table_ref[count + 2 * which]
            return dot(table, high) + dot(table_low, high) + dot(table, low)

        def right_back(value, which):
            high, low = parts_of(value)
            table = table_ref[2 * which + 1]
            table_low = table_ref[count + 2 * which + 1]
            return dot(high, table) + dot(high, table_low) + dot(low, table)

        re, im = join_rows(
            left_back(2, jnp.concatenate([re[:half], im[:half]], axis=0)),
            left_back(3, jnp.concatenate([re[half:], im[half:]], axis=0)),
        )
        mid_re, mid_im = join_lanes(
            right_back(jnp.concatenate([re[:, :half], im[:, :half]], axis=1), 2),
            right_back(jnp.concatenate([re[:, half:], im[:, half:]], axis=1), 3),
        )
        emit(
            last,
            wave_re * mid_re + wave_im * mid_im,
            wave_re * mid_im - wave_im * mid_re,
        )
        adj_buf[0] = win_re * mid_re + win_im * mid_im
        adj_buf[1] = win_im * mid_re - win_re * mid_im

        @pl.loop(1, depth_count)
        def backward(step):
            layer = last - step
            mid_re, mid_conj = propagate(adj_buf[0], adj_buf[1])
            win_re, win_im = window_of(layer)
            wave_re, wave_im = waves[layer, 0], waves[layer, 1]
            emit(
                layer,
                wave_re * mid_re - wave_im * mid_conj,
                -(wave_re * mid_conj + wave_im * mid_re),
            )
            adj_buf[0] = win_re * mid_re - win_im * mid_conj
            adj_buf[1] = win_im * mid_re + win_re * mid_conj

    def across_copy(part):
        return pltpu.make_async_remote_copy(
            src_ref=across.at[part], dst_ref=given.at[part], send_sem=send_f.at[part],
            recv_sem=recv_f.at[part], device_id=(me, opposite), device_id_type=MESH,
        )

    def across_scale_copy(part):
        return pltpu.make_async_remote_copy(
            src_ref=across_scale.at[part], dst_ref=given_scale.at[part],
            send_sem=send_fs.at[part], recv_sem=recv_fs.at[part], device_id=(me, opposite),
            device_id_type=MESH,
        )

    def share_copy(slot):
        return pltpu.make_async_remote_copy(
            src_ref=gin.at[slot], dst_ref=gin.at[share + slot], send_sem=send_h.at[slot],
            recv_sem=recv_g.at[share + slot], device_id=(me, partner), device_id_type=MESH,
        )

    def share_scale_copy(slot):
        return pltpu.make_async_remote_copy(
            src_ref=gin_scale.at[slot], dst_ref=gin_scale.at[share + slot],
            send_sem=send_hs.at[slot], recv_sem=recv_s.at[share + slot],
            device_id=(me, partner), device_id_type=MESH,
        )

    across_scale[...] = jnp.zeros(across_scale.shape, jnp.float32)
    for slot in range(share):
        pltpu.make_async_copy(gout.at[0], gin.at[slot], recv_g.at[slot]).wait()
        share_copy(slot).start()
        pltpu.make_async_copy(gscale.at[0], gin_scale.at[slot], recv_s.at[slot]).wait()
        share_scale_copy(slot).start()
    for slot in range(share):
        share_copy(slot).wait_recv()
        share_scale_copy(slot).wait_recv()
    places = [stripe * share + slot for slot in range(share)]
    places += [partner * share + slot for slot in range(share)]
    for part in range(2):
        own_sums, far_sums = [0.0] * 3, [0.0] * 3
        for slot in range(2 * share):
            owner, _, row, col = slot_of(places[slot])
            later = lax.rem(owner + 1, stripe_count)
            here = row_index >= row
            near = col_index >= col
            scale = gin_scale[slot, pl.ds(part, 1), :]
            left = gin[slot, part, :, pl.ds(0, half)].astype(jnp.int32).astype(jnp.float32)
            left = left * scale[:, :half]
            mid = gin[slot, part, :, pl.ds(half, half)].astype(jnp.int32).astype(jnp.float32)
            mid = mid * scale[:, half:]
            pieces = (jnp.where(near, left, 0.0), mid, jnp.where(near, 0.0, left))
            gain = [
                jnp.where(
                    here,
                    jnp.where(owner == target, 1.0, 0.0),
                    jnp.where(later == target, 1.0, 0.0),
                )
                for target in (stripe, opposite)
            ]
            for place, piece in enumerate(pieces):
                own_sums[place] = own_sums[place] + piece * gain[0]
                far_sums[place] = far_sums[place] + piece * gain[1]
        for place in range(3):
            lanes = pl.ds(place * half, half)
            most = jnp.max(jnp.abs(far_sums[place]), axis=0, keepdims=True)
            most = jnp.maximum(most, 1e-30)
            whole = jnp.round(far_sums[place] * (LEVELS / most)).astype(jnp.int32)
            across[part, :, lanes] = whole.astype(jnp.int16)
            across_scale[part, pl.ds(0, 1), lanes] = most * (1.0 / LEVELS)
            out_ref[0, part, :, lanes] = own_sums[place]
        across_copy(part).start()
        across_scale_copy(part).start()

    for part in range(2):
        across_copy(part).wait_recv()
        across_scale_copy(part).wait_recv()
        value = given[part].astype(jnp.int32).astype(jnp.float32)
        out_ref[0, part] += value * given_scale[part, pl.ds(0, 1), :]

    for part in range(2):
        for route in range(3):
            slab_copy(route, part).wait_send()
        across_copy(part).wait_send()
        across_scale_copy(part).wait_send()
    each_pattern_target(lambda copy: copy.wait_send())
    for slot in range(share):
        share_copy(slot).wait_send()
        share_scale_copy(slot).wait_send()
        target = worker_of(slot)

        @pl.when(me != target)
        def _():
            for part in range(2):
                window_copy(slot, part, target).wait_send()

    @pl.when(is_worker)
    def _():
        @pl.loop(0, depth_count)
        def drain(layer):
            @pl.when(layer != me)
            def _():
                grad_copy(layer).wait_send()
                scale_copy(layer).wait_send()


def body(tables, object_slices, probe_wave, amplitudes, positions, counts):
    stripe_count = lax.axis_size("stripe")
    depth_count = lax.axis_size("depth")
    layers, _, stripe_rows, width = object_slices.shape
    length = probe_wave.shape[1]
    capacity = amplitudes.shape[0]
    assert layers == 1 and stripe_rows == length and 2 * width == 3 * length
    share = capacity // 2
    assert depth_count >= 2 * (share + 2) and stripe_count == 4 and capacity % 2 == 0

    field = (2, length, length)
    slab = (2, stripe_rows, width)
    slab_scale = (2, 8, width)
    vmem = pl.BlockSpec(memory_space=pltpu.VMEM)
    smem = pl.BlockSpec(memory_space=pltpu.SMEM)
    dma = pltpu.SemaphoreType.DMA
    count = (tables.shape[0] - 2) // 4
    return pl.pallas_call(
        functools.partial(kernel, depth_count, stripe_count, capacity),
        out_shape=jax.ShapeDtypeStruct(object_slices.shape, jnp.float32),
        in_specs=[smem] * 2 + [vmem] * 4,
        out_specs=vmem,
        scratch_shapes=[
            pltpu.VMEM((stripe_count, stripe_rows, width), jnp.int16),
            pltpu.VMEM((stripe_count, stripe_rows, width), jnp.int16),
            pltpu.VMEM((share,) + field, jnp.int16),
            pltpu.VMEM((depth_count,) + field, jnp.int16),
            pltpu.VMEM((depth_count,) + field, jnp.float32),
            pltpu.VMEM((depth_count,) + field, jnp.int16),
            pltpu.VMEM((depth_count, 8, length), jnp.float32),
            pltpu.VMEM((2 * share,) + field, jnp.int16),
            pltpu.VMEM((2 * share, 8, length), jnp.float32),
            pltpu.VMEM((count, 3 * length, length), jnp.bfloat16),
            pltpu.VMEM((count, length, 3 * length), jnp.bfloat16),
            pltpu.VMEM(field, jnp.float32),
            pltpu.VMEM((stripe_count,) + amplitudes.shape, amplitudes.dtype),
            pltpu.VMEM(slab, jnp.int16),
            pltpu.VMEM(slab_scale, jnp.float32),
            pltpu.VMEM(slab, jnp.int16),
            pltpu.VMEM(slab_scale, jnp.float32),
            dma((3, 2)),
            dma((3, 2)),
            dma((share, 2)),
            dma((depth_count, 2)),
            dma((depth_count,)),
            dma((2 * share,)),
            dma((depth_count,)),
            dma((2 * share,)),
            dma((share,)),
            dma((share,)),
            dma((stripe_count // 2,)),
            dma((stripe_count,)),
            dma((2,)),
            dma((2,)),
            dma((2,)),
            dma((2,)),
        ],
        compiler_params=pltpu.CompilerParams(
            collective_id=0, has_side_effects=True, vmem_limit_bytes=60 * 1024 * 1024
        ),
    )(positions, counts, object_slices, probe_wave, amplitudes, tables)


def solution(mesh):
    def run(object_slices, probe_wave, amplitudes, positions, counts):
        tables = jnp.asarray(make_tables(probe_wave.shape[1]))
        return jax.shard_map(
            body,
            mesh=mesh,
            in_specs=(P(), P("depth", None, "stripe", None), P(), P("stripe", None, None), P(), P()),
            out_specs=P("depth", None, "stripe", None),
            check_vma=False,
        )(tables, object_slices, probe_wave, amplitudes, positions, counts)

    return run
```

```python
import functools

import jax
import jax.numpy as jnp
import numpy as np
from jax import lax
from jax.experimental import pallas as pl
from jax.experimental.pallas import tpu as pltpu
from jax.sharding import PartitionSpec as P

smoothing = 0.25
LEVELS = 32767.0
MESH = pl.DeviceIdType.MESH


def right_form(matrix):
    return np.block([[matrix.real, matrix.imag], [-matrix.imag, matrix.real]])


def make_tables(length):
    half = length // 2
    index = np.arange(length)
    dft = np.exp(-2j * np.pi * (np.outer(index, index) % length) / length) / np.sqrt(length)
    freq = (index + half) % length - half
    fresnel = np.exp(-1j * np.pi * freq.astype(np.float64) ** 2 / (2.0 * length))
    prop = dft.conj() @ (fresnel[:, None] * dft)
    first, second = prop[:half, :half], prop[:half, half:]
    parts = [(first + second) / 2, (first - second) / 2, dft[:half, 0::2], dft[:half, 1::2]]
    tables = []
    for part in parts:
        right = right_form(part)
        tables += [right, right.T]
    stacked = np.stack(tables).astype(np.float32)
    high = stacked.astype(jnp.bfloat16)
    low = (stacked - high.astype(np.float32)).astype(jnp.bfloat16)
    order = np.concatenate([np.arange(0, length, 2), np.arange(1, length, 2)])
    pick = np.zeros((length, length), np.float32)
    pick[np.arange(length), order] = 1.0
    picks = np.stack([pick, pick.T]).astype(jnp.bfloat16)
    return np.concatenate([high, low, picks], axis=0)


def parts_of(value):
    high = value.astype(jnp.bfloat16)
    low = (value - high.astype(jnp.float32)).astype(jnp.bfloat16)
    return high, low


def dot(a, b):
    return jnp.dot(a, b, preferred_element_type=jnp.float32)


def kernel(
    depth_count, stripe_count, capacity, positions_ref, counts_ref, object_ref, probe_ref, amp_ref,
    table_hbm, out_ref,
    slab_re, slab_im, win, wins, waves, gout, gscale, gin, gin_scale, rstack, lstack, adj_buf,
    table_ref, table_sem, patterns, across, across_scale, given, given_scale,
    send_n, recv_n, send_w, recv_w, send_g, recv_g, send_s, recv_s, send_h, send_hs, send_a, recv_a,
    send_f, recv_f, send_fs, recv_fs,
):
    me = lax.axis_index("depth")
    stripe = lax.axis_index("stripe")
    share = capacity // 2
    stride = depth_count // (share + 2)
    slabs = (slab_re, slab_im)
    length = probe_ref.shape[-1]
    half = length // 2
    count = (table_ref.shape[0] - 2) // 2
    partner = stripe + 1 - 2 * lax.rem(stripe, 2)
    opposite = lax.rem(stripe + 2, stripe_count)

    def slot_of(place):
        owner, passed, start = jnp.int32(0), jnp.int32(0), jnp.int32(0)
        for other in range(1, stripe_count):
            passed = passed + counts_ref[other - 1]
            owner = owner + jnp.where(place >= passed, 1, 0)
            start = jnp.where(place >= passed, passed, start)
        within = jnp.clip(place - start, 0, capacity - 1)
        slot = owner * capacity + within
        return owner, within, positions_ref[0, slot], positions_ref[1, slot]

    share_base = jnp.maximum(me - lax.rem(stripe, 2), 0)
    my_slot = jnp.clip(share_base // stride - 1, 0, share - 1)
    is_worker = me == (my_slot + 1) * stride + lax.rem(stripe, 2)

    @pl.when(is_worker)
    def _():
        pltpu.make_async_copy(table_hbm, table_ref, table_sem).start()

    barrier = pltpu.get_barrier_semaphore()

    @pl.loop(1, depth_count)
    def greet(step):
        other = lax.rem(me + step, depth_count)
        pl.semaphore_signal(barrier, inc=1, device_id=(other, stripe), device_id_type=MESH)

    for step in range(1, stripe_count):
        other = lax.rem(stripe + step, stripe_count)
        pl.semaphore_signal(barrier, inc=1, device_id=(me, other), device_id_type=MESH)
    for part in range(2):
        whole = jnp.round(object_ref[0, part] * LEVELS).astype(jnp.int32)
        slabs[part][stripe] = whole.astype(jnp.int16)
    pl.semaphore_wait(barrier, depth_count + stripe_count - 2)

    def slab_copy(route, part):
        source = opposite if route == 2 else stripe
        target = opposite if route == 1 else partner
        return pltpu.make_async_remote_copy(
            src_ref=slabs[part].at[source], dst_ref=slabs[part].at[source],
            send_sem=send_n.at[route, part], recv_sem=recv_n.at[route, part],
            device_id=(me, target), device_id_type=MESH,
        )

    for part in range(2):
        slab_copy(1, part).start()
        slab_copy(0, part).start()

    def worker_of(slot):
        return (slot + 1) * stride + lax.rem(stripe, 2)

    my_owner, my_within, my_row, my_col = slot_of(stripe * share + my_slot)

    def pattern_copy(parity, turn):
        return pltpu.make_async_remote_copy(
            src_ref=amp_ref, dst_ref=patterns.at[stripe], send_sem=send_a.at[turn],
            recv_sem=recv_a.at[stripe], device_id=(me, 2 * turn + parity), device_id_type=MESH,
        )

    def each_pattern_target(action):
        for parity in range(2):
            for slot in range(share):
                for turn in range(stripe_count // 2):
                    here = (me == (slot + 1) * stride + parity) & (stripe != 2 * turn + parity)

                    @pl.when(here)
                    def _():
                        action(pattern_copy(parity, turn))

    each_pattern_target(lambda copy: copy.start())

    for part in range(2):
        slab_copy(1, part).wait_recv()
        slab_copy(2, part).start()

    @pl.when(is_worker)
    def _():
        pltpu.make_async_copy(table_hbm, table_ref, table_sem).wait()
        for which in range(count // 2):
            high, low = table_ref[2 * which], table_ref[count + 2 * which]
            rstack[which] = jnp.concatenate([high, low, high], axis=0)
            high, low = table_ref[2 * which + 1], table_ref[count + 2 * which + 1]
            lstack[which] = jnp.concatenate([high, low, high], axis=1)
        gscale[...] = jnp.zeros(gscale.shape, jnp.float32)
        pltpu.make_async_copy(amp_ref, patterns.at[stripe], recv_a.at[stripe]).start()
        first = lax.broadcasted_iota(jnp.int32, (length, length), 0)
        second = lax.broadcasted_iota(jnp.int32, (length, length), 1)
        turned = second + my_row
        turned = jnp.where(turned >= length, turned - length, turned)
        turn_rows = jnp.where(first == turned, 1.0, 0.0).astype(jnp.bfloat16)
        turned = first + my_col
        turned = jnp.where(turned >= length, turned - length, turned)
        turn_cols = jnp.where(second == turned, 1.0, 0.0).astype(jnp.bfloat16)
        for part in range(2):
            value = dot(turn_rows, probe_ref[part]).astype(jnp.bfloat16)
            waves[0, part] = dot(value, turn_cols)

    def window_copy(slot, part, target):
        return pltpu.make_async_remote_copy(
            src_ref=win.at[slot, part], dst_ref=wins.at[me, part], send_sem=send_w.at[slot, part],
            recv_sem=recv_w.at[me, part], device_id=(target, stripe), device_id_type=MESH,
        )

    row_index = lax.broadcasted_iota(jnp.int32, (length, half), 0)
    col_index = lax.broadcasted_iota(jnp.int32, (length, half), 1)
    for part in range(2):
        slab_copy(0, part).wait_recv()
        slab_copy(2, part).wait_recv()
        for slot in range(share):
            owner, _, row, col = slot_of(stripe * share + slot)
            later = lax.rem(owner + 1, stripe_count)
            here = row_index >= row
            near = col_index >= col
            left, mid, right = (
                jnp.where(
                    here,
                    slabs[part][owner, :, pl.ds(place * half, half)].astype(jnp.int32),
                    slabs[part][later, :, pl.ds(place * half, half)].astype(jnp.int32),
                )
                for place in range(3)
            )
            win[slot, part, :, pl.ds(0, half)] = jnp.where(near, left, right).astype(jnp.int16)
            win[slot, part, :, pl.ds(half, half)] = mid.astype(jnp.int16)
            target = worker_of(slot)

            @pl.when(me != target)
            def _():
                window_copy(slot, part, target).start()

            @pl.when(me == target)
            def _():
                pltpu.make_async_copy(
                    win.at[slot, part], wins.at[me, part], recv_w.at[me, part]
                ).start()

    def wait_window(layer):
        for part in range(2):
            pltpu.make_async_copy(
                win.at[0, part], wins.at[layer, part], recv_w.at[layer, part]
            ).wait()

    def grad_copy(layer, part):
        return pltpu.make_async_remote_copy(
            src_ref=gout.at[layer, part], dst_ref=gin.at[my_slot, part],
            send_sem=send_g.at[layer, part], recv_sem=recv_g.at[my_slot, part], device_id=(layer, stripe), device_id_type=MESH,
        )

    def scale_copy(layer, part):
        return pltpu.make_async_remote_copy(
            src_ref=gscale.at[layer, part], dst_ref=gin_scale.at[my_slot, part],
            send_sem=send_s.at[layer, part], recv_sem=recv_s.at[my_slot, part], device_id=(layer, stripe), device_id_type=MESH,
        )

    def right_dot(value, which):
        high, low = parts_of(value)
        return dot(jnp.concatenate([high, high, low], axis=1), rstack[which])

    def left_dot(which, value):
        high, low = parts_of(value)
        return dot(lstack[which], jnp.concatenate([high, high, low], axis=0))

    def split_lanes(re, im):
        return (
            jnp.concatenate([re[:, :half] + re[:, half:], im[:, :half] + im[:, half:]], axis=1),
            jnp.concatenate([re[:, :half] - re[:, half:], im[:, :half] - im[:, half:]], axis=1),
        )

    def split_rows(re, im):
        return (
            jnp.concatenate([re[:half] + re[half:], im[:half] + im[half:]], axis=0),
            jnp.concatenate([re[:half] - re[half:], im[:half] - im[half:]], axis=0),
        )

    def join_lanes(p, q):
        return (
            jnp.concatenate([p[:, :half] + q[:, :half], p[:, :half] - q[:, :half]], axis=1),
            jnp.concatenate([p[:, half:] + q[:, half:], p[:, half:] - q[:, half:]], axis=1),
        )

    def join_rows(p, q):
        return (
            jnp.concatenate([p[:half] + q[:half], p[:half] - q[:half]], axis=0),
            jnp.concatenate([p[half:] + q[half:], p[half:] - q[half:]], axis=0),
        )

    def propagate(re, im):
        u, v = split_lanes(re, im)
        re, im = join_lanes(right_dot(u, 0), right_dot(v, 1))
        u, v = split_rows(re, im)
        return join_rows(left_dot(0, u), left_dot(1, v))

    def window_of(layer):
        value = wins[layer].astype(jnp.int32).astype(jnp.float32) * (1.0 / LEVELS)
        return value[0], value[1]

    def emit(layer, re, im):
        for part, value in enumerate((re, im)):
            most = jnp.max(jnp.abs(value), axis=0, keepdims=True)
            most = jnp.maximum(most, 1e-30)
            gout[layer, part] = jnp.round(value * (LEVELS / most)).astype(jnp.int32).astype(jnp.int16)
            gscale[layer, part, pl.ds(0, 1), :] = most * (1.0 / LEVELS)

            @pl.when(layer != me)
            def _():
                grad_copy(layer, part).start()
                scale_copy(layer, part).start()

            @pl.when(layer == me)
            def _():
                pltpu.make_async_copy(
                    gout.at[layer, part], gin.at[my_slot, part], recv_g.at[my_slot, part]
                ).start()
                pltpu.make_async_copy(
                    gscale.at[layer, part], gin_scale.at[my_slot, part], recv_s.at[my_slot, part]
                ).start()

    @pl.when(is_worker)
    def _():
        @pl.loop(0, depth_count - 1)
        def forward(layer):
            wait_window(layer)
            win_re, win_im = window_of(layer)
            re, im = waves[layer, 0], waves[layer, 1]
            re, im = propagate(re * win_re - im * win_im, re * win_im + im * win_re)
            waves[layer + 1, 0] = re
            waves[layer + 1, 1] = im

        last = depth_count - 1
        wait_window(last)
        win_re, win_im = window_of(last)
        wave_re, wave_im = waves[last, 0], waves[last, 1]
        re = wave_re * win_re - wave_im * win_im
        im = wave_re * win_im + wave_im * win_re
        u, v = split_lanes(re, im)
        even, odd = right_dot(u, 2), right_dot(v, 3)
        re = jnp.concatenate([even[:, :half], odd[:, :half]], axis=1)
        im = jnp.concatenate([even[:, half:], odd[:, half:]], axis=1)
        u, v = split_rows(re, im)
        even, odd = left_dot(2, u), left_dot(3, v)
        for source in range(stripe_count):
            pltpu.make_async_copy(amp_ref, patterns.at[source], recv_a.at[source]).wait()
        pick_rows, pick_cols = table_ref[2 * count], table_ref[2 * count + 1]
        amp = dot(dot(pick_rows, patterns[my_owner, my_within]).astype(jnp.bfloat16), pick_cols)
        re = jnp.concatenate([even[:half], odd[:half]], axis=0)
        im = jnp.concatenate([even[half:], odd[half:]], axis=0)
        factor = 1.0 - amp / jnp.sqrt(re * re + im * im + smoothing)
        re, im = factor * re, factor * im
        def left_back(which, value):
            high, low = parts_of(value)
            table = table_ref[2 * which]
            table_low = table_ref[count + 2 * which]
            return dot(table, high) + dot(table_low, high) + dot(table, low)

        def right_back(value, which):
            high, low = parts_of(value)
            table = table_ref[2 * which + 1]
            table_low = table_ref[count + 2 * which + 1]
            return dot(high, table) + dot(high, table_low) + dot(low, table)

        re, im = join_rows(
            left_back(2, jnp.concatenate([re[:half], im[:half]], axis=0)),
            left_back(3, jnp.concatenate([re[half:], im[half:]], axis=0)),
        )
        mid_re, mid_im = join_lanes(
            right_back(jnp.concatenate([re[:, :half], im[:, :half]], axis=1), 2),
            right_back(jnp.concatenate([re[:, half:], im[:, half:]], axis=1), 3),
        )
        emit(
            last,
            wave_re * mid_re + wave_im * mid_im,
            wave_re * mid_im - wave_im * mid_re,
        )
        adj_buf[0] = win_re * mid_re + win_im * mid_im
        adj_buf[1] = win_im * mid_re - win_re * mid_im

        @pl.loop(1, depth_count)
        def backward(step):
            layer = last - step
            mid_re, mid_conj = propagate(adj_buf[0], adj_buf[1])
            win_re, win_im = window_of(layer)
            wave_re, wave_im = waves[layer, 0], waves[layer, 1]
            emit(
                layer,
                wave_re * mid_re - wave_im * mid_conj,
                -(wave_re * mid_conj + wave_im * mid_re),
            )
            adj_buf[0] = win_re * mid_re - win_im * mid_conj
            adj_buf[1] = win_im * mid_re + win_re * mid_conj

    def across_copy(part):
        return pltpu.make_async_remote_copy(
            src_ref=across.at[part], dst_ref=given.at[part], send_sem=send_f.at[part],
            recv_sem=recv_f.at[part], device_id=(me, opposite), device_id_type=MESH,
        )

    def across_scale_copy(part):
        return pltpu.make_async_remote_copy(
            src_ref=across_scale.at[part], dst_ref=given_scale.at[part],
            send_sem=send_fs.at[part], recv_sem=recv_fs.at[part], device_id=(me, opposite),
            device_id_type=MESH,
        )

    def share_copy(slot, part):
        return pltpu.make_async_remote_copy(
            src_ref=gin.at[slot, part], dst_ref=gin.at[share + slot, part],
            send_sem=send_h.at[slot, part], recv_sem=recv_g.at[share + slot, part],
            device_id=(me, partner), device_id_type=MESH,
        )

    def share_scale_copy(slot, part):
        return pltpu.make_async_remote_copy(
            src_ref=gin_scale.at[slot, part], dst_ref=gin_scale.at[share + slot, part],
            send_sem=send_hs.at[slot, part], recv_sem=recv_s.at[share + slot, part],
            device_id=(me, partner), device_id_type=MESH,
        )

    across_scale[...] = jnp.zeros(across_scale.shape, jnp.float32)
    places = [stripe * share + slot for slot in range(share)]
    places += [partner * share + slot for slot in range(share)]
    for part in range(2):
        for slot in range(share):
            pltpu.make_async_copy(
                gout.at[0, part], gin.at[slot, part], recv_g.at[slot, part]
            ).wait()
            share_copy(slot, part).start()
            pltpu.make_async_copy(
                gscale.at[0, part], gin_scale.at[slot, part], recv_s.at[slot, part]
            ).wait()
            share_scale_copy(slot, part).start()
        for slot in range(share):
            share_copy(slot, part).wait_recv()
            share_scale_copy(slot, part).wait_recv()
        own_sums, far_sums = [0.0] * 3, [0.0] * 3
        for slot in range(2 * share):
            owner, _, row, col = slot_of(places[slot])
            later = lax.rem(owner + 1, stripe_count)
            here = row_index >= row
            near = col_index >= col
            scale = gin_scale[slot, part, pl.ds(0, 1), :]
            left = gin[slot, part, :, pl.ds(0, half)].astype(jnp.int32).astype(jnp.float32)
            left = left * scale[:, :half]
            mid = gin[slot, part, :, pl.ds(half, half)].astype(jnp.int32).astype(jnp.float32)
            mid = mid * scale[:, half:]
            pieces = (jnp.where(near, left, 0.0), mid, jnp.where(near, 0.0, left))
            gain = [
                jnp.where(
                    here,
                    jnp.where(owner == target, 1.0, 0.0),
                    jnp.where(later == target, 1.0, 0.0),
                )
                for target in (stripe, opposite)
            ]
            for place, piece in enumerate(pieces):
                own_sums[place] = own_sums[place] + piece * gain[0]
                far_sums[place] = far_sums[place] + piece * gain[1]
        for place in range(3):
            lanes = pl.ds(place * half, half)
            most = jnp.max(jnp.abs(far_sums[place]), axis=0, keepdims=True)
            most = jnp.maximum(most, 1e-30)
            whole = jnp.round(far_sums[place] * (LEVELS / most)).astype(jnp.int32)
            across[part, :, lanes] = whole.astype(jnp.int16)
            across_scale[part, pl.ds(0, 1), lanes] = most * (1.0 / LEVELS)
            out_ref[0, part, :, lanes] = own_sums[place]
        across_copy(part).start()
        across_scale_copy(part).start()

    for part in range(2):
        across_copy(part).wait_recv()
        across_scale_copy(part).wait_recv()
        value = given[part].astype(jnp.int32).astype(jnp.float32)
        out_ref[0, part] += value * given_scale[part, pl.ds(0, 1), :]

    for part in range(2):
        for route in range(3):
            slab_copy(route, part).wait_send()
        across_copy(part).wait_send()
        across_scale_copy(part).wait_send()
    each_pattern_target(lambda copy: copy.wait_send())
    for slot in range(share):
        for part in range(2):
            share_copy(slot, part).wait_send()
            share_scale_copy(slot, part).wait_send()
        target = worker_of(slot)

        @pl.when(me != target)
        def _():
            for part in range(2):
                window_copy(slot, part, target).wait_send()

    @pl.when(is_worker)
    def _():
        @pl.loop(0, depth_count)
        def drain(layer):
            @pl.when(layer != me)
            def _():
                for part in range(2):
                    grad_copy(layer, part).wait_send()
                    scale_copy(layer, part).wait_send()


def body(tables, object_slices, probe_wave, amplitudes, positions, counts):
    stripe_count = lax.axis_size("stripe")
    depth_count = lax.axis_size("depth")
    layers, _, stripe_rows, width = object_slices.shape
    length = probe_wave.shape[1]
    capacity = amplitudes.shape[0]
    assert layers == 1 and stripe_rows == length and 2 * width == 3 * length
    share = capacity // 2
    assert depth_count >= 2 * (share + 2) and stripe_count == 4 and capacity % 2 == 0

    field = (2, length, length)
    slab = (2, stripe_rows, width)
    slab_scale = (2, 8, width)
    vmem = pl.BlockSpec(memory_space=pltpu.VMEM)
    smem = pl.BlockSpec(memory_space=pltpu.SMEM)
    dma = pltpu.SemaphoreType.DMA
    count = (tables.shape[0] - 2) // 4
    return pl.pallas_call(
        functools.partial(kernel, depth_count, stripe_count, capacity),
        out_shape=jax.ShapeDtypeStruct(object_slices.shape, jnp.float32),
        in_specs=[smem] * 2 + [vmem] * 3 + [pl.BlockSpec(memory_space=pl.ANY)],
        out_specs=vmem,
        scratch_shapes=[
            pltpu.VMEM((stripe_count, stripe_rows, width), jnp.int16),
            pltpu.VMEM((stripe_count, stripe_rows, width), jnp.int16),
            pltpu.VMEM((share,) + field, jnp.int16),
            pltpu.VMEM((depth_count,) + field, jnp.int16),
            pltpu.VMEM((depth_count,) + field, jnp.float32),
            pltpu.VMEM((depth_count,) + field, jnp.int16),
            pltpu.VMEM((depth_count, 2, 8, length), jnp.float32),
            pltpu.VMEM((2 * share,) + field, jnp.int16),
            pltpu.VMEM((2 * share, 2, 8, length), jnp.float32),
            pltpu.VMEM((count, 3 * length, length), jnp.bfloat16),
            pltpu.VMEM((count, length, 3 * length), jnp.bfloat16),
            pltpu.VMEM(field, jnp.float32),
            pltpu.VMEM(tables.shape, tables.dtype),
            dma,
            pltpu.VMEM((stripe_count,) + amplitudes.shape, amplitudes.dtype),
            pltpu.VMEM(slab, jnp.int16),
            pltpu.VMEM(slab_scale, jnp.float32),
            pltpu.VMEM(slab, jnp.int16),
            pltpu.VMEM(slab_scale, jnp.float32),
            dma((3, 2)),
            dma((3, 2)),
            dma((share, 2)),
            dma((depth_count, 2)),
            dma((depth_count, 2)),
            dma((2 * share, 2)),
            dma((depth_count, 2)),
            dma((2 * share, 2)),
            dma((share, 2)),
            dma((share, 2)),
            dma((stripe_count // 2,)),
            dma((stripe_count,)),
            dma((2,)),
            dma((2,)),
            dma((2,)),
            dma((2,)),
        ],
        compiler_params=pltpu.CompilerParams(
            collective_id=0, has_side_effects=True, vmem_limit_bytes=60 * 1024 * 1024
        ),
    )(positions.T, counts, object_slices, probe_wave, amplitudes, tables)


def solution(mesh):
    def run(object_slices, probe_wave, amplitudes, positions, counts):
        tables = jnp.asarray(make_tables(probe_wave.shape[1]))
        return jax.shard_map(
            body,
            mesh=mesh,
            in_specs=(P(), P("depth", None, "stripe", None), P(), P("stripe", None, None), P(), P()),
            out_specs=P("depth", None, "stripe", None),
            check_vma=False,
        )(tables, object_slices, probe_wave, amplitudes, positions, counts)

    return run
```
